1024 devices in a mesh: ctx: 64 (over x, z_lo, core), tp: 8 (over y), pp: 2 (over z_hi).
Axes of the slice: x: 8, y: 8, z: 8 (z_hi: 2, z_lo: 4; z = z_hi * 4 + z_lo), core: 2. Of those that a mesh axis runs over, the one named last changes fastest.
Arguments:
- queries: bfloat16 [2, 8192, 8192], P('pp', 'ctx', 'tp'), may hold values from -6 to 6
- key_feats: bfloat16 [2, 8192, 8192], P('pp', 'ctx', 'tp'), may hold values from -6 to 6
- value_feats: bfloat16 [2, 8192, 8192], P('pp', 'ctx', 'tp'), may hold values from -6 to 6
- cotangent: bfloat16 [2, 8192, 8192], P('pp', 'ctx', 'tp'), may hold values from -70 to 70
- filters: float32 [2, 512, 128], P('pp', 'tp'), may hold values from -0.5 to 0.5
Outputs:
- grad_queries: bfloat16 [2, 8192, 8192], P('pp', 'ctx', 'tp')
- grad_keys: bfloat16 [2, 8192, 8192], P('pp', 'ctx', 'tp')
- handed: bfloat16 [2, 8192, 8192], P('pp', 'ctx', 'tp')
- grad_filters: float32 [2, 512, 128], P('pp', 'tp')
The draws below stay inside these ranges and needn't reach their ends.
All inputs are finite; a program needn't handle non-finite values.
Results may differ from the reference program's by a relative error of at most 0.0058.
Values may be sent and summed in bfloat16 or wider, within the bound.
No kernel may reach another device: no remote copies, remote signals or barrier semaphores. Data moves between devices by JAX's collectives and lax.ppermute only.
A program may use at most 64 MiB of HBM per device.

```python
import math
import jax
import jax.numpy as jnp
from jax import lax

D = 8192
TAPS = 128
GROUP = 16
GROUPS = 512
TOKENS = 8192
N_PP = 2


def draw_cotangent(key, part):
    keys = jax.random.split(key, 3)
    token_pos = jnp.arange(TOKENS, dtype=jnp.float32) / TOKENS
    channel_pos = jnp.arange(D, dtype=jnp.float32) / D
    col_scale = 10.0 ** (0.5 * channel_pos + 0.5 * jax.random.uniform(keys[2], (D,), jnp.float32))
    base = jnp.clip(jax.random.normal(keys[0], (N_PP, TOKENS, D), jnp.float32), -6.0, 6.0)
    row_scale = 10.0 ** (0.5 * token_pos + 0.5 * jax.random.uniform(keys[1], (TOKENS,), jnp.float32))
    values = base * row_scale[None, :, None] * col_scale[None, None, :] / 10.0
    return values.astype(jnp.bfloat16)


def levels(rng, shape, cuts, least, high):
    loudness = 1.0
    for dim, blocks in cuts:
        heights = jax.random.uniform(jax.random.fold_in(jax.random.fold_in(rng, 6), dim), (blocks,), jnp.float32, least / len(cuts), high / len(cuts))
        loudness = loudness * jnp.repeat(jnp.exp(heights), shape[dim] // blocks).reshape((-1,) + (1,) * (len(shape) - 1 - dim))
    return loudness


def scatter_about(own_key, extent, deviation, most, cuts=(), kind=jnp.bfloat16):
    values = jax.random.normal(own_key, extent, jnp.float32) * deviation
    if len(cuts) > 0:
        values = levels(own_key, extent, cuts, -0.22, 0.18) * values
    return jnp.clip(values, min=-most, max=most).astype(kind)


def setup_inputs(seed: int = 0) -> dict:
    key_list = jax.random.split(jax.random.key(seed), 6)
    queries = scatter_about(key_list[0], (N_PP, TOKENS, D), 1.0, 6.0, ((0, 2), (1, 64), (2, 8)))
    key_feats = scatter_about(key_list[1], (N_PP, TOKENS, D), 1.0, 6.0, ((0, 2), (1, 64), (2, 8)))
    value_feats = scatter_about(key_list[2], (N_PP, TOKENS, D), 1.0, 6.0, ((0, 2), (1, 64), (2, 8)))
    cotangent = draw_cotangent(jax.random.fold_in(key_list[5], 71), 0)
    filters = scatter_about(key_list[4], (N_PP, GROUPS, TAPS), TAPS ** -0.5, 0.5, ((0, 2), (1, 8)), jnp.float32)
    return dict(queries=queries, key_feats=key_feats, value_feats=value_feats, cotangent=cotangent, filters=filters)


def column_block(queries, key_feats, value_feats, cotangent, taps_bf):
    channels = queries.shape[1]
    per_channel = jnp.repeat(taps_bf.astype(jnp.float32), GROUP, axis=0).T
    product = (key_feats.astype(jnp.float32) * value_feats.astype(jnp.float32)).astype(jnp.bfloat16)
    product_f = product.astype(jnp.float32)
    zero_rim = jnp.zeros((TAPS - 1, channels), jnp.float32)
    padded_front = jnp.concatenate([zero_rim, product_f], axis=0)

    def fwd_step(tap_index, running):
        return running + per_channel[tap_index] * lax.dynamic_slice_in_dim(padded_front, TAPS - 1 - tap_index, TOKENS, 0)
    mixed = lax.fori_loop(0, TAPS, fwd_step, jnp.zeros((TOKENS, channels), jnp.float32))
    grad_q = (cotangent.astype(jnp.float32) * mixed).astype(jnp.bfloat16)
    weighted = (cotangent.astype(jnp.float32) * queries.astype(jnp.float32)).astype(jnp.bfloat16)
    weighted_f = weighted.astype(jnp.float32)
    padded_back = jnp.concatenate([weighted_f, zero_rim], axis=0)

    def back_step(tap_index, running):
        return running + per_channel[tap_index] * lax.dynamic_slice_in_dim(padded_back, tap_index, TOKENS, 0)
    dproduct = lax.fori_loop(0, TAPS, back_step, jnp.zeros((TOKENS, channels), jnp.float32))
    grad_k = (dproduct * value_feats.astype(jnp.float32)).astype(jnp.bfloat16)
    dvalues = (dproduct * key_feats.astype(jnp.float32)).astype(jnp.bfloat16)

    def tap_sum(tap_index):
        return lax.optimization_barrier(jnp.sum(weighted_f * lax.dynamic_slice_in_dim(padded_front, TAPS - 1 - tap_index, TOKENS, 0), axis=0))
    per_tap = lax.map(tap_sum, jnp.arange(TAPS))
    raw_grad = per_tap.reshape(TAPS, channels // GROUP, GROUP).sum(axis=2).T
    return (grad_q, grad_k, dvalues, raw_grad)

def reference(queries, key_feats, value_feats, cotangent, filters):
    channels = min(D, 512)
    num_blocks = D // channels

    def split(array):
        return array.reshape(TOKENS, num_blocks, channels).transpose(1, 0, 2)

    def merge(array):
        return array.transpose(1, 0, 2).reshape(TOKENS, D)
    grads_q = []
    grads_k = []
    values_all = []
    raw_all = []
    for section in range(N_PP):
        taps_bf = filters[section].astype(jnp.bfloat16).reshape(num_blocks, channels // GROUP, TAPS)
        results = lax.map(lambda pieces: column_block(*pieces), (split(queries[section]), split(key_feats[section]), split(value_feats[section]), split(cotangent[section]), taps_bf))
        grads_q.append(merge(results[0]))
        grads_k.append(merge(results[1]))
        values_all.append(merge(results[2]))
        raw_all.append(results[3].reshape(GROUPS, TAPS))
    grad_queries = jnp.stack(grads_q)
    grad_keys = jnp.stack(grads_k)
    dvalues = jnp.stack(values_all)
    handed = jnp.concatenate([dvalues[1:], jnp.zeros_like(dvalues[:1])], axis=0)
    raw_grad = jnp.stack(raw_all)
    total_norm = jnp.sqrt(jnp.sum(raw_grad * raw_grad))
    clip_level = 0.25 * math.sqrt(N_PP * GROUPS * TAPS)
    factor = jnp.minimum(1.0, clip_level / (total_norm + 1e-06))
    grad_filters = raw_grad * factor
    return (grad_queries, grad_keys, handed, grad_filters)
```

```python
import math

import jax
import jax.numpy as jnp
from jax import lax
from jax.experimental import pallas as pl
from jax.experimental.pallas import tpu as pltpu
from jax.sharding import Mesh, PartitionSpec as P


TAPS = 128
GROUP = 16
GROUPS = 512
LANES = 128
PER_BLOCK = LANES // GROUP

CTX = ("x", "zl", "core")
BF16 = jnp.bfloat16
F32 = jnp.float32


def flip_rows():
    row = lax.broadcasted_iota(jnp.int32, (LANES, LANES), 0)
    col = lax.broadcasted_iota(jnp.int32, (LANES, LANES), 1)
    return (row + col == LANES - 1).astype(F32).astype(BF16)


def dot(a, b):
    return jnp.dot(a, b, preferred_element_type=F32)


def products_kernel(k_ref, v_ref, c_ref, q_ref, p_ref, w_ref):
    flip = flip_rows()
    prod = k_ref[...] * v_ref[...]
    p_ref[...] = dot(flip, prod).astype(BF16)
    w_ref[...] = c_ref[...] * q_ref[...]


def filter_grad_kernel(w_ref, p_ref, hp_ref, raw_ref, stacked):
    row = lax.broadcasted_iota(jnp.int32, (LANES, LANES), 0)
    col = lax.broadcasted_iota(jnp.int32, (LANES, LANES), 1)
    own = row + col >= LANES - 1
    for block in range(w_ref.shape[1] // LANES):
        lanes = pl.ds(block * LANES, LANES)
        w = w_ref[:, lanes]
        for g in range(PER_BLOCK):
            stacked[pl.ds(g * LANES, LANES), :] = jnp.where(
                col // GROUP == g, w, jnp.zeros_like(w)
            )
        both = jnp.concatenate([p_ref[:, lanes], hp_ref[:, lanes]], axis=0)
        pairs = lax.dot_general(
            stacked[...], both, (((1,), (1,)), ((), ())), preferred_element_type=F32
        )
        for g in range(PER_BLOCK):
            part = pairs[g * LANES : (g + 1) * LANES]
            part = jnp.where(own, part[:, :LANES], part[:, LANES:])
            part = pltpu.roll(part, 1, 1, stride=1, stride_axis=0)
            raw_ref[pl.ds(block * PER_BLOCK + g, 1), :] = jnp.sum(part, axis=0, keepdims=True)


def mix_kernel(
    taps_ref, w_ref, hw_ref, p_ref, hp_ref, c_ref, k_ref, v_ref, gq_ref, gk_ref, dv_ref, stacked
):
    row = lax.broadcasted_iota(jnp.int32, (LANES, LANES), 0)
    col = lax.broadcasted_iota(jnp.int32, (LANES, LANES), 1)
    upper = col >= row
    flip = flip_rows()
    for block in range(w_ref.shape[1] // LANES):
        lanes = pl.ds(block * LANES, LANES)
        for g in range(PER_BLOCK):
            taps = taps_ref[pl.ds(block * PER_BLOCK + g, 1), :]
            taps = taps.astype(BF16).astype(F32)
            circ = pltpu.roll(
                jnp.broadcast_to(taps, (LANES, LANES)), 0, 1, stride=1, stride_axis=0
            )
            zero = jnp.zeros_like(circ)
            rows = pl.ds(g * LANES, LANES)
            stacked[rows, pl.ds(0, LANES)] = jnp.where(upper, circ, zero).astype(BF16)
            stacked[rows, pl.ds(LANES, LANES)] = jnp.where(upper, zero, circ).astype(BF16)
        data = jnp.concatenate(
            [
                jnp.concatenate([w_ref[:, lanes], p_ref[:, lanes]], axis=1),
                jnp.concatenate([hw_ref[:, lanes], hp_ref[:, lanes]], axis=1),
            ],
            axis=0,
        )
        out = dot(stacked[...], data)
        back = out[:LANES, :LANES]
        ahead = out[:LANES, LANES:]
        for g in range(1, PER_BLOCK):
            mine = col // GROUP == g
            back = jnp.where(mine, out[g * LANES : (g + 1) * LANES, :LANES], back)
            ahead = jnp.where(mine, out[g * LANES : (g + 1) * LANES, LANES:], ahead)
        gk_ref[:, lanes] = (back * v_ref[:, lanes].astype(F32)).astype(BF16)
        dv_ref[:, lanes] = (back * k_ref[:, lanes].astype(F32)).astype(BF16)
        cot = dot(flip, c_ref[:, lanes])
        gq_ref[:, lanes] = dot(flip, (cot * ahead).astype(BF16)).astype(BF16)


def exchange(rows, axes):
    return lax.all_to_all(rows, axes, 0, 0, tiled=True)


def per_device(queries, key_feats, value_feats, cotangent, filters):
    outs = block(queries[0], key_feats[0], value_feats[0], cotangent[0], filters[0])
    return tuple(out[None] for out in outs)


def block(q, k, v, c, filters):
    length, channels = q.shape
    groups_here = filters.shape[0]
    whole = jax.ShapeDtypeStruct((length, channels), BF16)
    size = length * channels * 2

    prod, weighted = pl.pallas_call(
        products_kernel,
        out_shape=(whole, whole),
        cost_estimate=pl.CostEstimate(
            flops=2 * LANES * length * channels, bytes_accessed=6 * size, transcendentals=0
        ),
    )(k, v, c, q)

    count = lax.axis_size(CTX)
    behind = lax.ppermute(prod, CTX, [(i, i + 1) for i in range(count - 1)])
    ahead = lax.ppermute(weighted, CTX, [(i + 1, i) for i in range(count - 1)])

    raw = pl.pallas_call(
        filter_grad_kernel,
        out_shape=jax.ShapeDtypeStruct((groups_here, TAPS), F32),
        scratch_shapes=[pltpu.VMEM((PER_BLOCK * LANES, LANES), BF16)],
        cost_estimate=pl.CostEstimate(
            flops=4 * groups_here * LANES**3, bytes_accessed=3 * size, transcendentals=0
        ),
    )(weighted, prod, behind)

    grad_q, grad_k, dvalues = pl.pallas_call(
        mix_kernel,
        out_shape=(whole, whole, whole),
        scratch_shapes=[pltpu.VMEM((PER_BLOCK * LANES, 2 * LANES), BF16)],
        cost_estimate=pl.CostEstimate(
            flops=8 * groups_here * LANES**3, bytes_accessed=10 * size, transcendentals=0
        ),
    )(filters, weighted, ahead, prod, behind, c, k, v)
    handed = lax.ppermute(dvalues, "pp", [(1, 0)])

    near = lax.axis_size(("zl", "core"))
    share = groups_here // near
    part = exchange(raw, ("zl", "core"))
    part = jnp.sum(part.reshape(near, share, TAPS), axis=0)
    wide = lax.axis_size("x")
    part = jnp.tile(part, (wide, 1))
    part = exchange(part, "x")
    part = jnp.sum(part.reshape(wide, share, TAPS), axis=0)
    square = jnp.sum(part * part, axis=0, keepdims=True)
    square = jnp.tile(square, (lax.axis_size("tp"), 1))
    square = exchange(square, "tp")
    square = jnp.sum(square, axis=0, keepdims=True)
    line = ("pp", "zl", "core")
    packed = jnp.concatenate([part, square], axis=0)
    packed = jnp.broadcast_to(packed[None], (lax.axis_size(line), share + 1, TAPS))
    packed = lax.all_to_all(packed, line, 0, 0)
    norm_sq = jnp.sum(packed[:, share])
    clip_level = 0.25 * math.sqrt(lax.axis_size("pp") * GROUPS * TAPS)
    factor = jnp.minimum(1.0, clip_level / (jnp.sqrt(norm_sq) + 1e-06))
    summed = lax.dynamic_slice_in_dim(packed, lax.axis_index("pp") * near, near, 0)
    grad_f = summed[:, :share].reshape(groups_here, TAPS) * factor
    return grad_q, grad_k, handed, grad_f


def solution(mesh):
    split = Mesh(
        mesh.devices.reshape(-1, 4, 2, mesh.shape["tp"], mesh.shape["pp"]),
        ("x", "zl", "core", "tp", "pp"),
    )
    acts = P("pp", CTX, "tp")
    taps = P("pp", "tp", None)
    return jax.shard_map(
        per_device,
        mesh=split,
        in_specs=(acts, acts, acts, acts, taps),
        out_specs=(acts, acts, acts, taps),
        check_vma=False,
    )
```

```python
import functools
import math

import jax
import jax.numpy as jnp
from jax import lax
from jax.experimental import pallas as pl
from jax.experimental.pallas import tpu as pltpu
from jax.sharding import Mesh, PartitionSpec as P


TAPS = 128
GROUP = 16
GROUPS = 512
LANES = 128
PER_BLOCK = LANES // GROUP

CTX = ("x", "zl", "core")
VMEM_LIMIT = 16 * 1024 * 1024
BF16 = jnp.bfloat16
F32 = jnp.float32


def flip_rows():
    row = lax.broadcasted_iota(jnp.int32, (LANES, LANES), 0)
    col = lax.broadcasted_iota(jnp.int32, (LANES, LANES), 1)
    return (row + col == LANES - 1).astype(F32).astype(BF16)


def dot(a, b):
    return jnp.dot(a, b, preferred_element_type=F32)


def products_kernel(k_ref, v_ref, c_ref, q_ref, p_ref, w_ref):
    flip = flip_rows()
    prod = k_ref[...] * v_ref[...]
    p_ref[...] = dot(flip, prod).astype(BF16)
    w_ref[...] = c_ref[...] * q_ref[...]


def filter_grad_kernel(w_ref, p_ref, hp_ref, raw_ref, stacked):
    row = lax.broadcasted_iota(jnp.int32, (LANES, LANES), 0)
    col = lax.broadcasted_iota(jnp.int32, (LANES, LANES), 1)
    own = row + col >= LANES - 1
    for block in range(w_ref.shape[1] // LANES):
        lanes = pl.ds(block * LANES, LANES)
        w = w_ref[:, lanes]
        for g in range(PER_BLOCK):
            stacked[pl.ds(g * LANES, LANES), :] = jnp.where(
                col // GROUP == g, w, jnp.zeros_like(w)
            )
        both = jnp.concatenate([p_ref[:, lanes], hp_ref[:, lanes]], axis=0)
        pairs = lax.dot_general(
            stacked[...], both, (((1,), (1,)), ((), ())), preferred_element_type=F32
        )
        for g in range(PER_BLOCK):
            part = pairs[g * LANES : (g + 1) * LANES]
            part = jnp.where(own, part[:, :LANES], part[:, LANES:])
            part = pltpu.roll(part, 1, 1, stride=1, stride_axis=0)
            spot = pl.ds(g * (raw_ref.shape[0] // PER_BLOCK) + block, 1)
            raw_ref[spot, :] = jnp.sum(part, axis=0, keepdims=True)


def mix_kernel(
    taps_ref, w_ref, hw_ref, p_ref, hp_ref, c_ref, k_ref, v_ref, gq_ref, gk_ref, dv_ref, stacked
):
    row = lax.broadcasted_iota(jnp.int32, (LANES, LANES), 0)
    col = lax.broadcasted_iota(jnp.int32, (LANES, LANES), 1)
    upper = col >= row
    flip = flip_rows()
    for block in range(w_ref.shape[1] // LANES):
        lanes = pl.ds(block * LANES, LANES)
        for g in range(PER_BLOCK):
            taps = taps_ref[pl.ds(block * PER_BLOCK + g, 1), :]
            taps = taps.astype(BF16).astype(F32)
            circ = pltpu.roll(
                jnp.broadcast_to(taps, (LANES, LANES)), 0, 1, stride=1, stride_axis=0
            )
            zero = jnp.zeros_like(circ)
            rows = pl.ds(g * LANES, LANES)
            stacked[rows, pl.ds(0, LANES)] = jnp.where(upper, circ, zero).astype(BF16)
            stacked[rows, pl.ds(LANES, LANES)] = jnp.where(upper, zero, circ).astype(BF16)
        data = jnp.concatenate(
            [
                jnp.concatenate([w_ref[:, lanes], p_ref[:, lanes]], axis=1),
                jnp.concatenate([hw_ref[:, lanes], hp_ref[:, lanes]], axis=1),
            ],
            axis=0,
        )
        out = dot(stacked[...], data)
        back = out[:LANES, :LANES]
        ahead = out[:LANES, LANES:]
        for g in range(1, PER_BLOCK):
            mine = col // GROUP == g
            back = jnp.where(mine, out[g * LANES : (g + 1) * LANES, :LANES], back)
            ahead = jnp.where(mine, out[g * LANES : (g + 1) * LANES, LANES:], ahead)
        gk_ref[:, lanes] = (back * v_ref[:, lanes].astype(F32)).astype(BF16)
        dv_ref[:, lanes] = (back * k_ref[:, lanes].astype(F32)).astype(BF16)
        cot = dot(flip, c_ref[:, lanes])
        gq_ref[:, lanes] = dot(flip, (cot * ahead).astype(BF16)).astype(BF16)


def settle_kernel(*refs):
    half = len(refs) // 2
    for in_ref, out_ref in zip(refs[:half], refs[half:]):
        out_ref[...] = in_ref[...]


def settle(*arrays):
    size = sum(a.size * a.dtype.itemsize for a in arrays)
    return pl.pallas_call(
        settle_kernel,
        out_shape=tuple(jax.ShapeDtypeStruct(a.shape, a.dtype) for a in arrays),
        compiler_params=pltpu.CompilerParams(vmem_limit_bytes=VMEM_LIMIT),
        cost_estimate=pl.CostEstimate(flops=0, bytes_accessed=2 * size, transcendentals=0),
    )(*[near_in(a) for a in arrays])


def pack_kernel(part_ref, squares_ref, packed_ref):
    squares = jnp.sum(squares_ref[...], axis=0, keepdims=True)
    share, taps = part_ref.shape
    for member in range(packed_ref.shape[0]):
        for row in range(share):
            packed_ref[member, :, pl.ds(row * taps, taps)] = part_ref[pl.ds(row, 1), :]
        packed_ref[member, :, pl.ds(share * taps, taps)] = squares


def clip_kernel(clip_level, packed_ref, grad_ref):
    members, _, width = packed_ref.shape
    squares = packed_ref[0, :, pl.ds(width - TAPS, TAPS)]
    for member in range(1, members):
        squares += packed_ref[member, :, pl.ds(width - TAPS, TAPS)]
    norm = jnp.sqrt(jnp.sum(squares, axis=1, keepdims=True))
    factor = jnp.minimum(1.0, clip_level / (norm + 1e-06))
    near = members // lax.axis_size("pp")
    first = lax.axis_index("pp") * near
    for row in range(width // TAPS - 1):
        for member in range(near):
            own = packed_ref[first + member, :, pl.ds(row * TAPS, TAPS)]
            grad_ref[pl.ds(row * near + member, 1), :] = own * factor


def near_in(x):
    return pltpu.with_memory_space_constraint(x, pltpu.VMEM)


def exchange(rows, axes):
    return lax.all_to_all(rows, axes, 0, 0, tiled=True)


def per_device(queries, key_feats, value_feats, cotangent, filters):
    outs = block(queries[0], key_feats[0], value_feats[0], cotangent[0], filters[0])
    return tuple(out[None] for out in outs)


def block(q, k, v, c, filters):
    length, channels = q.shape
    groups_here = filters.shape[0]
    inner = pltpu.VMEM((length, channels), BF16)
    size = length * channels * 2

    prod, weighted = pl.pallas_call(
        products_kernel,
        out_shape=(inner, inner),
        cost_estimate=pl.CostEstimate(
            flops=2 * LANES * length * channels, bytes_accessed=6 * size, transcendentals=0
        ),
    )(k, v, c, q)

    count = lax.axis_size(CTX)
    behind = lax.ppermute(prod, CTX, [(i, i + 1) for i in range(count - 1)])
    ahead = lax.ppermute(weighted, CTX, [(i + 1, i) for i in range(count - 1)])

    raw = pl.pallas_call(
        filter_grad_kernel,
        out_shape=pltpu.VMEM((groups_here, TAPS), F32),
        scratch_shapes=[pltpu.VMEM((PER_BLOCK * LANES, LANES), BF16)],
        compiler_params=pltpu.CompilerParams(vmem_limit_bytes=VMEM_LIMIT),
        cost_estimate=pl.CostEstimate(
            flops=4 * groups_here * LANES**3, bytes_accessed=3 * size, transcendentals=0
        ),
    )(near_in(weighted), near_in(prod), near_in(behind))

    grad_q, grad_k, dvalues = pl.pallas_call(
        mix_kernel,
        out_shape=(inner, inner, inner),
        scratch_shapes=[pltpu.VMEM((PER_BLOCK * LANES, 2 * LANES), BF16)],
        compiler_params=pltpu.CompilerParams(vmem_limit_bytes=VMEM_LIMIT),
        cost_estimate=pl.CostEstimate(
            flops=8 * groups_here * LANES**3, bytes_accessed=10 * size, transcendentals=0
        ),
    )(filters, near_in(weighted), near_in(ahead), near_in(prod), near_in(behind), near_in(c), near_in(k), near_in(v))
    handed = lax.ppermute(dvalues, "pp", [(1, 0)])
    (handed,) = settle(handed)
    grad_q, grad_k = settle(grad_q, grad_k)

    near = lax.axis_size(("zl", "core"))
    share = groups_here // near
    part = exchange(raw, ("zl", "core"))
    part = jnp.sum(part.reshape(near, share, TAPS), axis=0)
    wide = lax.axis_size("x")
    part = jnp.tile(part, (wide, 1))
    part = exchange(part, "x")
    part = jnp.sum(part.reshape(wide, share, TAPS), axis=0)
    squares = jnp.sum(part * part, axis=0, keepdims=True)
    squares = jnp.tile(squares, (lax.axis_size("tp"), 1))
    squares = exchange(squares, "tp")
    line = ("pp", "zl", "core")
    members = lax.axis_size(line)
    packed = pl.pallas_call(
        pack_kernel,
        out_shape=jax.ShapeDtypeStruct((members, 1, (share + 1) * TAPS), F32),
        compiler_params=pltpu.CompilerParams(vmem_limit_bytes=VMEM_LIMIT),
    )(near_in(part), near_in(squares))
    packed = lax.all_to_all(packed, line, 0, 0, tiled=True)
    clip_level = 0.25 * math.sqrt(lax.axis_size("pp") * GROUPS * TAPS)
    grad_f = pl.pallas_call(
        functools.partial(clip_kernel, clip_level),
        out_shape=jax.ShapeDtypeStruct((groups_here, TAPS), F32),
        compiler_params=pltpu.CompilerParams(vmem_limit_bytes=VMEM_LIMIT),
    )(near_in(packed))
    return grad_q, grad_k, handed, grad_f


def solution(mesh):
    split = Mesh(
        mesh.devices.reshape(-1, 4, 2, mesh.shape["tp"], mesh.shape["pp"]),
        ("x", "zl", "core", "tp", "pp"),
    )
    acts = P("pp", CTX, "tp")
    taps = P("pp", "tp", None)
    return jax.shard_map(
        per_device,
        mesh=split,
        in_specs=(acts, acts, acts, acts, taps),
        out_specs=(acts, acts, acts, taps),
        check_vma=False,
    )
```

```python
import functools
import math

import jax
import jax.numpy as jnp
from jax import lax
from jax.experimental import pallas as pl
from jax.experimental.pallas import tpu as pltpu
from jax.sharding import Mesh, PartitionSpec as P


TAPS = 128
GROUP = 16
GROUPS = 512
LANES = 128
PER_BLOCK = LANES // GROUP

CTX = ("x", "zl", "core")
VMEM_LIMIT = 16 * 1024 * 1024
BF16 = jnp.bfloat16
F32 = jnp.float32


def flip_rows():
    row = lax.broadcasted_iota(jnp.int32, (LANES, LANES), 0)
    col = lax.broadcasted_iota(jnp.int32, (LANES, LANES), 1)
    return (row + col == LANES - 1).astype(F32).astype(BF16)


def dot(a, b):
    return jnp.dot(a, b, preferred_element_type=F32)


def products_kernel(k_ref, v_ref, c_ref, q_ref, p_ref, w_ref):
    flip = flip_rows()
    prod = k_ref[...] * v_ref[...]
    p_ref[...] = dot(flip, prod).astype(BF16)
    w_ref[...] = c_ref[...] * q_ref[...]


def filter_grad_kernel(w_ref, p_ref, hp_ref, raw_ref, stacked):
    row = lax.broadcasted_iota(jnp.int32, (LANES, LANES), 0)
    col = lax.broadcasted_iota(jnp.int32, (LANES, LANES), 1)
    own = row + col >= LANES - 1
    for block in range(w_ref.shape[1] // LANES):
        lanes = pl.ds(block * LANES, LANES)
        w = w_ref[:, lanes]
        for g in range(PER_BLOCK):
            stacked[pl.ds(g * LANES, LANES), :] = jnp.where(
                col // GROUP == g, w, jnp.zeros_like(w)
            )
        both = jnp.concatenate([p_ref[:, lanes], hp_ref[:, lanes]], axis=0)
        pairs = lax.dot_general(
            stacked[...], both, (((1,), (1,)), ((), ())), preferred_element_type=F32
        )
        for g in range(PER_BLOCK):
            part = pairs[g * LANES : (g + 1) * LANES]
            part = jnp.where(own, part[:, :LANES], part[:, LANES:])
            part = pltpu.roll(part, 1, 1, stride=1, stride_axis=0)
            spot = pl.ds(g * (raw_ref.shape[0] // PER_BLOCK) + block, 1)
            raw_ref[spot, :] = jnp.sum(part, axis=0, keepdims=True)


def mix_kernel(
    taps_ref, w_ref, hw_ref, p_ref, hp_ref, c_ref, k_ref, v_ref, gq_ref, gk_ref, dv_ref, stacked
):
    row = lax.broadcasted_iota(jnp.int32, (LANES, LANES), 0)
    col = lax.broadcasted_iota(jnp.int32, (LANES, LANES), 1)
    upper = col >= row
    flip = flip_rows()
    for block in range(w_ref.shape[1] // LANES):
        lanes = pl.ds(block * LANES, LANES)
        for g in range(PER_BLOCK):
            taps = taps_ref[pl.ds(block * PER_BLOCK + g, 1), :]
            taps = taps.astype(BF16).astype(F32)
            circ = pltpu.roll(
                jnp.broadcast_to(taps, (LANES, LANES)), 0, 1, stride=1, stride_axis=0
            )
            zero = jnp.zeros_like(circ)
            rows = pl.ds(g * LANES, LANES)
            stacked[rows, pl.ds(0, LANES)] = jnp.where(upper, circ, zero).astype(BF16)
            stacked[rows, pl.ds(LANES, LANES)] = jnp.where(upper, zero, circ).astype(BF16)
        data = jnp.concatenate(
            [
                jnp.concatenate([w_ref[:, lanes], p_ref[:, lanes]], axis=1),
                jnp.concatenate([hw_ref[:, lanes], hp_ref[:, lanes]], axis=1),
            ],
            axis=0,
        )
        out = dot(stacked[...], data)
        back = out[:LANES, :LANES]
        ahead = out[:LANES, LANES:]
        for g in range(1, PER_BLOCK):
            mine = col // GROUP == g
            back = jnp.where(mine, out[g * LANES : (g + 1) * LANES, :LANES], back)
            ahead = jnp.where(mine, out[g * LANES : (g + 1) * LANES, LANES:], ahead)
        gk_ref[:, lanes] = (back * v_ref[:, lanes].astype(F32)).astype(BF16)
        dv_ref[:, lanes] = (back * k_ref[:, lanes].astype(F32)).astype(BF16)
        cot = dot(flip, c_ref[:, lanes])
        gq_ref[:, lanes] = dot(flip, (cot * ahead).astype(BF16)).astype(BF16)


def settle_kernel(*refs):
    half = len(refs) // 2
    for in_ref, out_ref in zip(refs[:half], refs[half:]):
        out_ref[...] = in_ref[...]


def settle(*arrays):
    size = sum(a.size * a.dtype.itemsize for a in arrays)
    return pl.pallas_call(
        settle_kernel,
        out_shape=tuple(jax.ShapeDtypeStruct(a.shape, a.dtype) for a in arrays),
        compiler_params=pltpu.CompilerParams(vmem_limit_bytes=VMEM_LIMIT),
        cost_estimate=pl.CostEstimate(flops=0, bytes_accessed=2 * size, transcendentals=0),
    )(*[near_in(a) for a in arrays])


def pack_kernel(part_ref, squares_ref, packed_ref):
    squares = jnp.sum(squares_ref[...], axis=0, keepdims=True)
    share, taps = part_ref.shape
    for member in range(packed_ref.shape[0]):
        for row in range(share):
            packed_ref[member, :, pl.ds(row * taps, taps)] = part_ref[pl.ds(row, 1), :]
        packed_ref[member, :, pl.ds(share * taps, taps)] = squares


def clip_kernel(clip_level, packed_ref, grad_ref):
    members, _, width = packed_ref.shape
    squares = packed_ref[0, :, pl.ds(width - TAPS, TAPS)]
    for member in range(1, members):
        squares += packed_ref[member, :, pl.ds(width - TAPS, TAPS)]
    norm = jnp.sqrt(jnp.sum(squares, axis=1, keepdims=True))
    factor = jnp.minimum(1.0, clip_level / (norm + 1e-06))
    near = members // lax.axis_size("pp")
    first = members - near - lax.axis_index("pp") * near
    for row in range(width // TAPS - 1):
        for member in range(near):
            own = packed_ref[first + member, :, pl.ds(row * TAPS, TAPS)]
            grad_ref[pl.ds(row * near + member, 1), :] = own * factor


def near_in(x):
    return pltpu.with_memory_space_constraint(x, pltpu.VMEM)


def exchange(rows, axes, order):
    return lax.all_to_all(rows, axes, 0, 0, tiled=True, axis_index_groups=[order])


def from_middle(count):
    return [(count // 2 + i) % count for i in range(count)]


def per_device(queries, key_feats, value_feats, cotangent, filters):
    outs = block(queries[0], key_feats[0], value_feats[0], cotangent[0], filters[0])
    return tuple(out[None] for out in outs)


def block(q, k, v, c, filters):
    length, channels = q.shape
    groups_here = filters.shape[0]
    inner = pltpu.VMEM((length, channels), BF16)
    size = length * channels * 2

    prod, weighted = pl.pallas_call(
        products_kernel,
        out_shape=(inner, inner),
        cost_estimate=pl.CostEstimate(
            flops=2 * LANES * length * channels, bytes_accessed=6 * size, transcendentals=0
        ),
    )(k, v, c, q)

    count = lax.axis_size(CTX)
    behind = lax.ppermute(prod, CTX, [(i, i + 1) for i in range(count - 1)])
    ahead = lax.ppermute(weighted, CTX, [(i + 1, i) for i in range(count - 1)])

    raw = pl.pallas_call(
        filter_grad_kernel,
        out_shape=pltpu.VMEM((groups_here, TAPS), F32),
        scratch_shapes=[pltpu.VMEM((PER_BLOCK * LANES, LANES), BF16)],
        compiler_params=pltpu.CompilerParams(vmem_limit_bytes=VMEM_LIMIT),
        cost_estimate=pl.CostEstimate(
            flops=4 * groups_here * LANES**3, bytes_accessed=3 * size, transcendentals=0
        ),
    )(near_in(weighted), near_in(prod), near_in(behind))

    grad_q, grad_k, dvalues = pl.pallas_call(
        mix_kernel,
        out_shape=(inner, inner, inner),
        scratch_shapes=[pltpu.VMEM((PER_BLOCK * LANES, 2 * LANES), BF16)],
        compiler_params=pltpu.CompilerParams(vmem_limit_bytes=VMEM_LIMIT),
        cost_estimate=pl.CostEstimate(
            flops=8 * groups_here * LANES**3, bytes_accessed=10 * size, transcendentals=0
        ),
    )(filters, near_in(weighted), near_in(ahead), near_in(prod), near_in(behind), near_in(c), near_in(k), near_in(v))
    handed = lax.ppermute(dvalues, "pp", [(1, 0)])
    (handed,) = settle(handed)
    grad_q, grad_k = settle(grad_q, grad_k)

    near = lax.axis_size(("zl", "core"))
    share = groups_here // near
    cores = lax.axis_size("core")
    by_near = [zl * cores + core for zl in (1, 2, 0, 3) for core in range(cores)]
    part = exchange(raw, ("zl", "core"), by_near)
    part = jnp.sum(part.reshape(near, share, TAPS), axis=0)
    wide = lax.axis_size("x")
    part = jnp.tile(part, (wide, 1))
    part = exchange(part, "x", from_middle(wide))
    part = jnp.sum(part.reshape(wide, share, TAPS), axis=0)
    squares = jnp.sum(part * part, axis=0, keepdims=True)
    deep = lax.axis_size("tp")
    squares = jnp.tile(squares, (deep, 1))
    squares = exchange(squares, "tp", from_middle(deep))
    line = ("pp", "zl", "core")
    members = lax.axis_size(line)
    packed = pl.pallas_call(
        pack_kernel,
        out_shape=jax.ShapeDtypeStruct((members, 1, (share + 1) * TAPS), F32),
        compiler_params=pltpu.CompilerParams(vmem_limit_bytes=VMEM_LIMIT),
    )(near_in(part), near_in(squares))
    halves = reversed(range(lax.axis_size("pp")))
    packed = exchange(packed, line, [pp * near + i for pp in halves for i in by_near])
    clip_level = 0.25 * math.sqrt(lax.axis_size("pp") * GROUPS * TAPS)
    grad_f = pl.pallas_call(
        functools.partial(clip_kernel, clip_level),
        out_shape=jax.ShapeDtypeStruct((groups_here, TAPS), F32),
        compiler_params=pltpu.CompilerParams(vmem_limit_bytes=VMEM_LIMIT),
    )(near_in(packed))
    return grad_q, grad_k, handed, grad_f


def solution(mesh):
    split = Mesh(
        mesh.devices.reshape(-1, 4, 2, mesh.shape["tp"], mesh.shape["pp"]),
        ("x", "zl", "core", "tp", "pp"),
    )
    acts = P("pp", CTX, "tp")
    taps = P("pp", "tp", None)
    return jax.shard_map(
        per_device,
        mesh=split,
        in_specs=(acts, acts, acts, acts, taps),
        out_specs=(acts, acts, acts, taps),
        check_vma=False,
    )
```

```python
import functools
import math

import jax
import jax.numpy as jnp
from jax import lax
from jax.experimental import pallas as pl
from jax.experimental.pallas import tpu as pltpu
from jax.sharding import Mesh, PartitionSpec as P


TAPS = 128
GROUP = 16
GROUPS = 512
LANES = 128
PER_BLOCK = LANES // GROUP

CTX = ("x", "zl", "core")
VMEM_LIMIT = 16 * 1024 * 1024
BF16 = jnp.bfloat16
F32 = jnp.float32


def flip_rows():
    row = lax.broadcasted_iota(jnp.int32, (LANES, LANES), 0)
    col = lax.broadcasted_iota(jnp.int32, (LANES, LANES), 1)
    return (row + col == LANES - 1).astype(F32).astype(BF16)


def dot(a, b):
    return jnp.dot(a, b, preferred_element_type=F32)


def products_kernel(k_ref, v_ref, c_ref, q_ref, p_ref, w_ref):
    flip = flip_rows()
    prod = k_ref[...] * v_ref[...]
    p_ref[...] = dot(flip, prod).astype(BF16)
    w_ref[...] = c_ref[...] * q_ref[...]


def filter_grad_kernel(w_ref, p_ref, hp_ref, raw_ref, stacked):
    row = lax.broadcasted_iota(jnp.int32, (LANES, LANES), 0)
    col = lax.broadcasted_iota(jnp.int32, (LANES, LANES), 1)
    own = row + col >= LANES - 1
    for block in range(w_ref.shape[1] // LANES):
        lanes = pl.ds(block * LANES, LANES)
        w = w_ref[:, lanes]
        for g in range(PER_BLOCK):
            stacked[pl.ds(g * LANES, LANES), :] = jnp.where(
                col // GROUP == g, w, jnp.zeros_like(w)
            )
        both = jnp.concatenate([p_ref[:, lanes], hp_ref[:, lanes]], axis=0)
        pairs = lax.dot_general(
            stacked[...], both, (((1,), (1,)), ((), ())), preferred_element_type=F32
        )
        for g in range(PER_BLOCK):
            part = pairs[g * LANES : (g + 1) * LANES]
            part = jnp.where(own, part[:, :LANES], part[:, LANES:])
            part = pltpu.roll(part, 1, 1, stride=1, stride_axis=0)
            spot = pl.ds(g * (raw_ref.shape[0] // PER_BLOCK) + block, 1)
            raw_ref[spot, :] = jnp.sum(part, axis=0, keepdims=True)


def mix_kernel(
    taps_ref, w_ref, hw_ref, p_ref, hp_ref, c_ref, k_ref, v_ref, gq_ref, gk_ref, dv_ref, stacked
):
    row = lax.broadcasted_iota(jnp.int32, (LANES, LANES), 0)
    col = lax.broadcasted_iota(jnp.int32, (LANES, LANES), 1)
    upper = col >= row
    flip = flip_rows()
    for block in range(w_ref.shape[1] // LANES):
        lanes = pl.ds(block * LANES, LANES)
        for g in range(PER_BLOCK):
            taps = taps_ref[pl.ds(block * PER_BLOCK + g, 1), :]
            taps = taps.astype(BF16).astype(F32)
            circ = pltpu.roll(
                jnp.broadcast_to(taps, (LANES, LANES)), 0, 1, stride=1, stride_axis=0
            )
            zero = jnp.zeros_like(circ)
            rows = pl.ds(g * LANES, LANES)
            stacked[rows, pl.ds(0, LANES)] = jnp.where(upper, circ, zero).astype(BF16)
            stacked[rows, pl.ds(LANES, LANES)] = jnp.where(upper, zero, circ).astype(BF16)
        data = jnp.concatenate(
            [
                jnp.concatenate([w_ref[:, lanes], p_ref[:, lanes]], axis=1),
                jnp.concatenate([hw_ref[:, lanes], hp_ref[:, lanes]], axis=1),
            ],
            axis=0,
        )
        out = dot(stacked[...], data)
        back = out[:LANES, :LANES]
        ahead = out[:LANES, LANES:]
        for g in range(1, PER_BLOCK):
            mine = col // GROUP == g
            back = jnp.where(mine, out[g * LANES : (g + 1) * LANES, :LANES], back)
            ahead = jnp.where(mine, out[g * LANES : (g + 1) * LANES, LANES:], ahead)
        gk_ref[:, lanes] = (back * v_ref[:, lanes].astype(F32)).astype(BF16)
        dv_ref[:, lanes] = (back * k_ref[:, lanes].astype(F32)).astype(BF16)
        cot = dot(flip, c_ref[:, lanes])
        gq_ref[:, lanes] = dot(flip, (cot * ahead).astype(BF16)).astype(BF16)


def pack_kernel(part_ref, squares_ref, packed_ref):
    squares = jnp.sum(squares_ref[...], axis=0, keepdims=True)
    share, taps = part_ref.shape
    for member in range(packed_ref.shape[0]):
        for row in range(share):
            packed_ref[member, :, pl.ds(row * taps, taps)] = part_ref[pl.ds(row, 1), :]
        packed_ref[member, :, pl.ds(share * taps, taps)] = squares


def clip_kernel(clip_level, by_near, packed_ref, *refs):
    count = (len(refs) - 2) // 2
    grad_ref, sems = refs[count], refs[-1]
    copies = [
        pltpu.make_async_copy(refs[i], refs[count + 1 + i], sems.at[i]) for i in range(count)
    ]
    for copy in copies:
        copy.start()
    members, _, width = packed_ref.shape
    squares = packed_ref[0, :, pl.ds(width - TAPS, TAPS)]
    for member in range(1, members):
        squares += packed_ref[member, :, pl.ds(width - TAPS, TAPS)]
    norm = jnp.sqrt(jnp.sum(squares, axis=1, keepdims=True))
    factor = jnp.minimum(1.0, clip_level / (norm + 1e-06))
    near = members // lax.axis_size("pp")
    first = members - near - lax.axis_index("pp") * near
    for row in range(width // TAPS - 1):
        for member in range(near):
            own = packed_ref[first + member, :, pl.ds(row * TAPS, TAPS)]
            grad_ref[pl.ds(row * near + by_near.index(member), 1), :] = own * factor
    for copy in copies:
        copy.wait()


def near_in(x):
    return pltpu.with_memory_space_constraint(x, pltpu.VMEM)


def exchange(rows, axes, order):
    return lax.all_to_all(rows, axes, 0, 0, tiled=True, axis_index_groups=[order])


def from_middle(count):
    return [(count // 2 + i) % count for i in range(count)]


def per_device(queries, key_feats, value_feats, cotangent, filters):
    outs = block(queries[0], key_feats[0], value_feats[0], cotangent[0], filters[0])
    return tuple(out[None] for out in outs)


def block(q, k, v, c, filters):
    length, channels = q.shape
    groups_here = filters.shape[0]
    inner = pltpu.VMEM((length, channels), BF16)
    size = length * channels * 2

    prod, weighted = pl.pallas_call(
        products_kernel,
        out_shape=(inner, inner),
        cost_estimate=pl.CostEstimate(
            flops=2 * LANES * length * channels, bytes_accessed=6 * size, transcendentals=0
        ),
    )(k, v, c, q)

    count = lax.axis_size(CTX)
    behind = lax.ppermute(prod, CTX, [(i, i + 1) for i in range(count - 1)])
    ahead = lax.ppermute(weighted, CTX, [(i + 1, i) for i in range(count - 1)])

    raw = pl.pallas_call(
        filter_grad_kernel,
        out_shape=pltpu.VMEM((groups_here, TAPS), F32),
        scratch_shapes=[pltpu.VMEM((PER_BLOCK * LANES, LANES), BF16)],
        compiler_params=pltpu.CompilerParams(vmem_limit_bytes=VMEM_LIMIT),
        cost_estimate=pl.CostEstimate(
            flops=4 * groups_here * LANES**3, bytes_accessed=3 * size, transcendentals=0
        ),
    )(near_in(weighted), near_in(prod), near_in(behind))

    grad_q, grad_k, dvalues = pl.pallas_call(
        mix_kernel,
        out_shape=(inner, inner, inner),
        scratch_shapes=[pltpu.VMEM((PER_BLOCK * LANES, 2 * LANES), BF16)],
        compiler_params=pltpu.CompilerParams(vmem_limit_bytes=VMEM_LIMIT),
        cost_estimate=pl.CostEstimate(
            flops=8 * groups_here * LANES**3, bytes_accessed=10 * size, transcendentals=0
        ),
    )(filters, near_in(weighted), near_in(ahead), near_in(prod), near_in(behind), near_in(c), near_in(k), near_in(v))
    handed = lax.ppermute(dvalues, "pp", [(1, 0)])
    near = lax.axis_size(("zl", "core"))
    share = groups_here // near
    cores = lax.axis_size("core")
    by_near = [zl * cores + core for zl in (2, 1, 3, 0) for core in range(cores)]
    part = exchange(raw, ("zl", "core"), by_near)
    part = jnp.sum(part.reshape(near, share, TAPS), axis=0)
    wide = lax.axis_size("x")
    part = jnp.tile(part, (wide, 1))
    part = exchange(part, "x", from_middle(wide))
    part = jnp.sum(part.reshape(wide, share, TAPS), axis=0)
    squares = jnp.sum(part * part, axis=0, keepdims=True)
    deep = lax.axis_size("tp")
    squares = jnp.tile(squares, (deep, 1))
    squares = exchange(squares, "tp", from_middle(deep))
    line = ("pp", "zl", "core")
    members = lax.axis_size(line)
    packed = pl.pallas_call(
        pack_kernel,
        out_shape=jax.ShapeDtypeStruct((members, 1, (share + 1) * TAPS), F32),
        compiler_params=pltpu.CompilerParams(vmem_limit_bytes=VMEM_LIMIT),
    )(near_in(part), near_in(squares))
    halves = reversed(range(lax.axis_size("pp")))
    packed = exchange(packed, line, [pp * near + i for pp in halves for i in range(near)])
    clip_level = 0.25 * math.sqrt(lax.axis_size("pp") * GROUPS * TAPS)
    whole = jax.ShapeDtypeStruct((length, channels), BF16)
    grad_f, grad_q, grad_k, handed = pl.pallas_call(
        functools.partial(clip_kernel, clip_level, by_near),
        out_shape=(jax.ShapeDtypeStruct((groups_here, TAPS), F32), whole, whole, whole),
        out_specs=(pl.BlockSpec(memory_space=pltpu.VMEM),)
        + (pl.BlockSpec(memory_space=pltpu.HBM),) * 3,
        scratch_shapes=[pltpu.SemaphoreType.DMA((3,))],
        compiler_params=pltpu.CompilerParams(vmem_limit_bytes=VMEM_LIMIT),
    )(near_in(packed), near_in(grad_q), near_in(grad_k), near_in(handed))
    return grad_q, grad_k, handed, grad_f


def solution(mesh):
    split = Mesh(
        mesh.devices.reshape(-1, 4, 2, mesh.shape["tp"], mesh.shape["pp"]),
        ("x", "zl", "core", "tp", "pp"),
    )
    acts = P("pp", CTX, "tp")
    taps = P("pp", "tp", None)
    return jax.shard_map(
        per_device,
        mesh=split,
        in_specs=(acts, acts, acts, acts, taps),
        out_specs=(acts, acts, acts, taps),
        check_vma=False,
    )
```
